32 devices in a mesh: groups: 2 (over x), tensor: 16 (over z, y, core).
Axes of the slice: x: 2, y: 2, z: 4, core: 2. Of those that a mesh axis runs over, the one named last changes fastest.
Arguments:
- gate_act: bfloat16 [53248, 32], P('tensor', 'groups'), parts along dimension 1, may hold values from -6 to 6
- up_act: bfloat16 [53248, 32], P('tensor', 'groups'), parts along dimension 1, may hold values from -6 to 6
- codes: int32 [26624, 8192], P('tensor'), may hold values from 0 to 255
- scales: bfloat16 [1664, 8192], P('tensor'), may hold values from 0.00039863586 to 0.0015945435
Outputs:
- ffn_out: bfloat16 [32, 8192], P(('groups', 'tensor')), parts along dimension 0
The draws below stay inside these ranges and needn't reach their ends.
There are 2 independent parts, one for each index of `groups`. The reference program is written for one: setup_inputs(seed, part) draws one part's arguments, and reference() takes and returns one part's arrays. A program takes and returns all parts, laid end to end along the dimension named above; an argument that names none is the same for every part. Nothing has to cross between parts.
Inputs may be any that keep to these rules, and one draw needn't show every extreme that they name: Each word packs two 4-bit codes as stated in the reference program.
All inputs are finite; a program needn't handle non-finite values.
Results may differ from the reference program's by a relative error of at most 0.007.
Values may be sent and summed in bfloat16 or wider, within the bound.
A program may use at most 384 MiB of HBM per device.

```python
import math
import jax
import jax.numpy as jnp
import numpy as np
from jax import lax

D = 8192
FF = 53248
HAD_CROSS = 128
GROUP = 32
HAD_LOCAL = 416
ROWS = 16


def touch_ends(result, key, least, top_value):
    longest = result.shape.index(max(result.shape))
    spots = []
    for shift in (0, 1):
        where = [jax.random.randint(jax.random.fold_in(key, axis), (), 0, length) for axis, length in enumerate(result.shape)]
        where[longest] = (where[longest] + shift) % result.shape[longest]
        spots.append(tuple(where))
    return result.at[spots[0]].set(least).at[spots[1]].set(top_value)


def shard_levels(own_key, shape, cuts, smallest, largest):
    def one(axis_at, blocks):
        heights = jax.random.uniform(jax.random.fold_in(jax.random.fold_in(own_key, 6), axis_at), (blocks,), jnp.float32, smallest / len(cuts), largest / len(cuts))
        return jnp.repeat(jnp.exp(heights), shape[axis_at] // blocks).reshape((-1,) + (1,) * (len(shape) - axis_at - 1))

    factor_of = one(*cuts[0])
    for cut in cuts[1:]:
        factor_of = factor_of * one(*cut)
    return factor_of


def scatter_about(rng, extent, width, limit, cuts=(), kind=jnp.bfloat16):
    result = width * jax.random.normal(rng, extent, jnp.float32)
    if cuts:
        result = result * shard_levels(rng, extent, cuts, -0.22, 0.18)
    return jnp.clip(result, -limit, limit).astype(kind)


def setup_inputs(seed: int = 0, part: int = 0) -> dict:
    streams_of = jax.random.split(jax.random.key(seed), 5)
    part_keys = jax.random.split(jax.random.fold_in(streams_of[4], part), 5)
    gate_act = scatter_about(part_keys[0], (FF, ROWS), 1.0, 6.0, ((0, 16),))
    up_act = scatter_about(part_keys[1], (FF, ROWS), 1.0, 6.0, ((0, 16),))
    codes = touch_ends(jax.random.randint(streams_of[2], (FF // 2, D), 0, 256), jax.random.fold_in(streams_of[2], 1), 0, 255).astype(jnp.int32)
    scales = jnp.clip(jnp.exp(math.log(0.0015945435) - 1.3862944 * jax.random.uniform(streams_of[3], (FF // GROUP, D), jnp.float32) ** shard_levels(streams_of[3], (FF // GROUP, D), ((0, 16),), -0.2, 0.2)), 0.00039863586, 0.0015945435).astype(jnp.bfloat16)
    return dict(gate_act=gate_act, up_act=up_act, codes=codes, scales=scales)


def paley_table():
    squares = set()
    for real_part in range(5):
        for root_part in range(5):
            squares.add(((real_part * real_part + 2 * root_part * root_part) % 5, 2 * real_part * root_part % 5))
    jacobsthal = np.zeros((25, 25))
    for first in range(25):
        for second in range(25):
            differ = ((first // 5 - second // 5) % 5, (first % 5 - second % 5) % 5)
            if differ == (0, 0):
                jacobsthal[first, second] = 0.0
            elif differ in squares:
                jacobsthal[first, second] = 1.0
            else:
                jacobsthal[first, second] = -1.0
    conference = np.zeros((26, 26))
    conference[0, 1:] = 1.0
    conference[1:, 0] = 1.0
    conference[1:, 1:] = jacobsthal
    return np.kron(conference, np.array([[1.0, 1.0], [1.0, -1.0]])) + np.kron(np.eye(26), np.array([[1.0, -1.0], [-1.0, -1.0]]))

def walsh_table(order):
    matrix = np.ones((1, 1))
    while matrix.shape[0] < order:
        matrix = np.kron(np.array([[1.0, 1.0], [1.0, -1.0]]), matrix)
    return matrix

def hadamard_local(order):
    matrix = np.kron(walsh_table(order // 52), paley_table()) / math.sqrt(order)
    return jnp.asarray(matrix, dtype=jnp.float32).astype(jnp.bfloat16)

def sign_table(order):
    row_index = jnp.arange(order, dtype=jnp.int32)[:, None]
    col_index = jnp.arange(order, dtype=jnp.int32)[None, :]
    shared = jnp.zeros((order, order), jnp.int32)
    for bit_pos in range(order.bit_length() - 1):
        shared = shared + row_index // 2 ** bit_pos % 2 * (col_index // 2 ** bit_pos % 2)
    return (1 - 2 * (shared % 2)).astype(jnp.float32)

def dequantize(words, group_scales):
    low_codes = words % 16
    high_codes = words // 16
    unpacked = jnp.stack([low_codes, high_codes], axis=1).reshape(2 * words.shape[0], words.shape[1])
    spread = jnp.repeat(group_scales.astype(jnp.float32), GROUP, axis=0)
    return ((unpacked - 8).astype(jnp.float32) * spread).astype(jnp.bfloat16)

def reference(gate_act, up_act, codes, scales):
    total_rows = gate_act.shape[1]
    hidden = (jax.nn.silu(gate_act.astype(jnp.float32)) * up_act.astype(jnp.float32)).astype(jnp.bfloat16)
    blocks = hidden.reshape(HAD_CROSS, HAD_LOCAL, total_rows)
    local_table = hadamard_local(HAD_LOCAL).astype(jnp.float32)
    local = jnp.einsum('kn,anr->akr', local_table, blocks.astype(jnp.float32), precision=lax.Precision.HIGHEST).astype(jnp.bfloat16)
    signs = sign_table(HAD_CROSS)
    rotated = (jnp.einsum('abr,ae->ebr', local.astype(jnp.float32), signs, precision=lax.Precision.HIGHEST) * (1.0 / math.sqrt(HAD_CROSS))).astype(jnp.bfloat16)
    word_blocks = codes.reshape(HAD_CROSS, HAD_LOCAL // 2, codes.shape[1])
    scale_blocks = scales.reshape(HAD_CROSS, HAD_LOCAL // GROUP, scales.shape[1])

    def advance(total, items):
        words, group_scales, values = items
        weight = dequantize(words, group_scales)
        return (total + jnp.dot(values.T, weight, preferred_element_type=jnp.float32), None)
    start = jnp.zeros((total_rows, codes.shape[1]), jnp.float32)
    total, unused = lax.scan(advance, start, (word_blocks, scale_blocks, rotated))
    return total.astype(jnp.bfloat16)
```

```python
import functools
import math

import jax
import jax.numpy as jnp
import numpy as np
from jax import lax
from jax.experimental import pallas as pl
from jax.experimental.pallas import tpu as pltpu
from jax.sharding import PartitionSpec as P

HAD_CROSS = 128
GROUP = 32
HAD_LOCAL = 416


def swapped(value, axis, distance):
    mask = 2**distance
    pairs = [(source, source ^ mask) for source in range(lax.axis_size(axis))]
    return lax.ppermute(value, axis, pairs)


def paley_table():
    squares = set()
    for real_part in range(5):
        for root_part in range(5):
            squares.add(
                (
                    (real_part * real_part + 2 * root_part * root_part) % 5,
                    2 * real_part * root_part % 5,
                )
            )
    jacobsthal = np.zeros((25, 25))
    for first in range(25):
        for second in range(25):
            differ = ((first // 5 - second // 5) % 5, (first % 5 - second % 5) % 5)
            if differ == (0, 0):
                jacobsthal[first, second] = 0.0
            elif differ in squares:
                jacobsthal[first, second] = 1.0
            else:
                jacobsthal[first, second] = -1.0
    conference = np.zeros((26, 26))
    conference[0, 1:] = 1.0
    conference[1:, 0] = 1.0
    conference[1:, 1:] = jacobsthal
    return np.kron(conference, np.array([[1.0, 1.0], [1.0, -1.0]])) + np.kron(
        np.eye(26), np.array([[1.0, -1.0], [-1.0, -1.0]])
    )


def walsh_table(order):
    matrix = np.ones((1, 1))
    while matrix.shape[0] < order:
        matrix = np.kron(np.array([[1.0, 1.0], [1.0, -1.0]]), matrix)
    return matrix


def hadamard_local(order):
    matrix = np.kron(walsh_table(order // 52), paley_table()) / math.sqrt(order)
    return jnp.asarray(matrix, dtype=jnp.float32).astype(jnp.bfloat16)


def sign_table(order):
    row_index = jnp.arange(order, dtype=jnp.int32)[:, None]
    col_index = jnp.arange(order, dtype=jnp.int32)[None, :]
    shared = jnp.zeros((order, order), jnp.int32)
    for bit_pos in range(order.bit_length() - 1):
        shared = shared + row_index // 2**bit_pos % 2 * (col_index // 2**bit_pos % 2)
    return (1 - 2 * (shared % 2)).astype(jnp.float32)


def dequantize(words, group_scales):
    low_codes = words % 16
    high_codes = words // 16
    unpacked = jnp.stack([low_codes, high_codes], axis=1).reshape(
        2 * words.shape[0], words.shape[1]
    )
    spread = jnp.repeat(group_scales.astype(jnp.float32), GROUP, axis=0)
    return ((unpacked - 8).astype(jnp.float32) * spread).astype(jnp.bfloat16)


def body(gate_act, up_act, codes, scales):
    units_here = gate_act.shape[0]
    total_rows = gate_act.shape[1]
    blocks_here = units_here // HAD_LOCAL
    factor = 1.0 / math.sqrt(HAD_CROSS)
    hidden = (jax.nn.silu(gate_act.astype(jnp.float32)) * up_act.astype(jnp.float32)).astype(
        jnp.bfloat16
    )
    hidden = hidden.reshape(blocks_here, HAD_LOCAL, total_rows)
    local_table = hadamard_local(HAD_LOCAL)
    local = jnp.einsum(
        "kn,anr->akr", local_table, hidden, preferred_element_type=jnp.float32
    ).astype(jnp.bfloat16)
    partial_sums = jnp.einsum(
        "abr,ae->ebr",
        local.astype(jnp.float32),
        sign_table(blocks_here),
        precision=lax.Precision.HIGHEST,
    )
    my_index = lax.axis_index("tensor")
    for bit_pos in range(lax.axis_size("tensor").bit_length() - 1):
        partner = swapped(partial_sums, "tensor", bit_pos)
        upper = my_index // 2**bit_pos % 2
        partial_sums = jnp.where(upper == 0, partial_sums + partner, partner - partial_sums)
    rotated = (partial_sums * factor).astype(jnp.bfloat16)
    rotated = rotated.reshape(units_here, total_rows)
    weight = dequantize(codes, scales)
    summed = lax.psum_scatter(
        lax.dot_general(
            rotated, weight, (((0,), (0,)), ((), ())), preferred_element_type=jnp.float32
        ),
        "tensor",
        scatter_dimension=0,
        tiled=True,
    )
    return summed.astype(jnp.bfloat16)


MESH = pl.DeviceIdType.MESH
CHUNK = 512
PAD = 512


def local_padded(order):
    matrix = np.kron(walsh_table(order // 52), paley_table()) / math.sqrt(order)
    half = order // 2
    table = np.zeros((order, PAD), np.float32)
    table[:, :half] = matrix[0::2].T
    table[:, PAD // 2 : PAD // 2 + half] = matrix[1::2].T
    return jnp.asarray(table).astype(jnp.bfloat16)


def swap_table(outer, inner):
    table = np.zeros((outer * inner, outer * inner), np.float32)
    for i in range(outer):
        for j in range(inner):
            table[j * outer + i, i * inner + j] = 1.0
    return jnp.asarray(table).astype(jnp.bfloat16)


def f32_dot(left, right):
    return jnp.dot(left, right, preferred_element_type=jnp.float32)


def fused_kernel(
    sizes,
    gate_ref, up_ref, codes_ref, scales_ref, table_ref, walsh_ref, swap1_ref, swap2_ref, swap3_ref,
    out_ref,
    words, scale16, scale32, snd1, rcv1, snd2, rcv2, rot, acc, snd3, rcv3,
    code_sem, scale_sem, send1, recv1, send2, recv2, send3, recv3,
):
    groups, ranks, blocks, chunks = sizes
    rows = groups * ranks
    half_words = HAD_LOCAL // 2
    bands = HAD_LOCAL // GROUP
    band = GROUP // 2
    my_group = lax.axis_index("groups")
    my_rank = lax.axis_index("tensor")
    me = my_group * ranks + my_rank
    base = my_group * (chunks * CHUNK)

    def code_copy(j):
        start = pl.multiple_of(base + j * CHUNK, CHUNK)
        return pltpu.make_async_copy(
            codes_ref.at[:, pl.ds(start, CHUNK)], words.at[j], code_sem.at[j]
        )

    scale_copy = pltpu.make_async_copy(
        scales_ref.at[:, pl.ds(pl.multiple_of(base, CHUNK), chunks * CHUNK)], scale16, scale_sem
    )
    scale_copy.start()

    @pl.loop(0, chunks)
    def _(j):
        code_copy(j).start()

    barrier = pltpu.get_barrier_semaphore()

    @pl.loop(1, rows)
    def _(k):
        peer = lax.rem(me + k, rows)
        pl.semaphore_signal(
            barrier, inc=1, device_id=(peer // ranks, lax.rem(peer, ranks)), device_id_type=MESH
        )

    table = table_ref[...]
    parts = []
    for a in range(blocks):
        gate = gate_ref[a * HAD_LOCAL : (a + 1) * HAD_LOCAL, :].astype(jnp.float32)
        up = up_ref[a * HAD_LOCAL : (a + 1) * HAD_LOCAL, :].astype(jnp.float32)
        hidden = (gate / (1.0 + jnp.exp(-gate)) * up).astype(jnp.bfloat16)
        parts.append(
            lax.dot_general(
                hidden, table, (((0,), (0,)), ((), ())), preferred_element_type=jnp.float32
            ).astype(jnp.bfloat16)
        )
    local = f32_dot(swap1_ref[...], jnp.concatenate(parts, axis=0))
    snd1[...] = local.reshape(ranks, blocks, PAD).astype(jnp.bfloat16)
    rcv1[my_rank] = snd1[my_rank]
    pl.semaphore_wait(barrier, rows - 1)

    def copy1(k):
        peer = lax.rem(my_rank + k, ranks)
        return pltpu.make_async_remote_copy(
            src_ref=snd1.at[peer], dst_ref=rcv1.at[my_rank],
            send_sem=send1.at[k], recv_sem=recv1.at[k],
            device_id=(my_group, peer), device_id_type=MESH,
        )

    @pl.loop(1, ranks)
    def _(k):
        copy1(k).start()

    scale_copy.wait()
    scale32[...] = scale16[...].astype(jnp.float32)

    @pl.loop(1, ranks)
    def _(k):
        copy1(k).wait()

    gathered = rcv1[...].astype(jnp.float32).reshape(ranks * blocks, PAD).astype(jnp.bfloat16)
    rotated = f32_dot(walsh_ref[...], gathered) * (1.0 / math.sqrt(HAD_CROSS))
    snd2[...] = rotated.reshape(ranks, blocks, PAD).astype(jnp.bfloat16)
    rcv2[me] = snd2[my_rank]

    def copy2(k):
        peer = lax.rem(me + k, rows)
        return pltpu.make_async_remote_copy(
            src_ref=snd2.at[lax.rem(peer, ranks)], dst_ref=rcv2.at[me],
            send_sem=send2.at[k], recv_sem=recv2.at[k],
            device_id=(peer // ranks, lax.rem(peer, ranks)), device_id_type=MESH,
        )

    @pl.loop(1, rows)
    def _(k):
        copy2(k).start()

    @pl.loop(1, rows)
    def _(k):
        copy2(k).wait()

    gathered = rcv2[...].astype(jnp.float32).reshape(rows * blocks, PAD).astype(jnp.bfloat16)
    rot[...] = f32_dot(swap2_ref[...], gathered).astype(jnp.bfloat16)

    gap = jnp.zeros((PAD // 2 - half_words, CHUNK), jnp.bfloat16)

    @pl.loop(0, chunks)
    def _(j):
        code_copy(j).wait()
        columns = pl.ds(pl.multiple_of(j * CHUNK, CHUNK), CHUNK)
        total = jnp.zeros((rows, CHUNK), jnp.float32)
        for a in range(blocks):
            low, high = [], []
            for n in range(bands):
                word = words[j, a * half_words + n * band : a * half_words + (n + 1) * band, :]
                row = a * bands + n
                scale = jnp.broadcast_to(scale32[row : row + 1, columns], (band, CHUNK)).astype(
                    jnp.bfloat16
                )
                low.append(((word & 15).astype(jnp.float32).astype(jnp.bfloat16) - 8) * scale)
                high.append(((word >> 4).astype(jnp.float32).astype(jnp.bfloat16) - 8) * scale)
            weight = jnp.concatenate(low + [gap] + high + [gap], axis=0)
            total = total + f32_dot(rot[a * rows : (a + 1) * rows, :], weight)
        acc[pl.ds(pl.multiple_of(j * rows, rows), rows), :] = total.astype(jnp.bfloat16)

    sums = f32_dot(swap3_ref[...], acc[...])
    snd3[...] = sums.reshape(rows, chunks, CHUNK).astype(jnp.bfloat16)
    rcv3[me] = snd3[me]

    def copy3(k):
        peer = lax.rem(me + k, rows)
        return pltpu.make_async_remote_copy(
            src_ref=snd3.at[peer], dst_ref=rcv3.at[me],
            send_sem=send3.at[k], recv_sem=recv3.at[k],
            device_id=(peer // ranks, lax.rem(peer, ranks)), device_id_type=MESH,
        )

    @pl.loop(1, rows)
    def _(k):
        copy3(k).start()

    @pl.loop(1, rows)
    def _(k):
        copy3(k).wait()

    for g in range(groups):
        out_ref[g] = jnp.sum(rcv3[g * ranks : (g + 1) * ranks].astype(jnp.float32), axis=0).astype(
            jnp.bfloat16
        )


def fused_body(gate_act, up_act, codes, scales):
    groups, ranks = lax.axis_size("groups"), lax.axis_size("tensor")
    rows = groups * ranks
    blocks = gate_act.shape[0] // HAD_LOCAL
    width = codes.shape[1]
    chunks = width // groups // CHUNK
    vmem = pl.BlockSpec(memory_space=pltpu.VMEM)
    hbm = pl.BlockSpec(memory_space=pl.ANY)
    bf16 = jnp.bfloat16
    walsh = jnp.asarray(walsh_table(HAD_CROSS), jnp.float32).astype(bf16)
    out = pl.pallas_call(
        functools.partial(fused_kernel, (groups, ranks, blocks, chunks)),
        out_shape=jax.ShapeDtypeStruct((groups, chunks, CHUNK), bf16),
        in_specs=[vmem, vmem, hbm, hbm] + [vmem] * 5,
        out_specs=vmem,
        scratch_shapes=[
            pltpu.VMEM((chunks, codes.shape[0], CHUNK), jnp.int32),
            pltpu.VMEM((scales.shape[0], chunks * CHUNK), bf16),
            pltpu.VMEM((scales.shape[0], chunks * CHUNK), jnp.float32),
            pltpu.VMEM((ranks, blocks, PAD), bf16),
            pltpu.VMEM((ranks, blocks, PAD), bf16),
            pltpu.VMEM((ranks, blocks, PAD), bf16),
            pltpu.VMEM((rows, blocks, PAD), bf16),
            pltpu.VMEM((blocks * rows, PAD), bf16),
            pltpu.VMEM((chunks * rows, CHUNK), bf16),
            pltpu.VMEM((rows, chunks, CHUNK), bf16),
            pltpu.VMEM((rows, chunks, CHUNK), bf16),
            pltpu.SemaphoreType.DMA((chunks,)),
            pltpu.SemaphoreType.DMA,
            pltpu.SemaphoreType.DMA((ranks,)),
            pltpu.SemaphoreType.DMA((ranks,)),
            pltpu.SemaphoreType.DMA((rows,)),
            pltpu.SemaphoreType.DMA((rows,)),
            pltpu.SemaphoreType.DMA((rows,)),
            pltpu.SemaphoreType.DMA((rows,)),
        ],
        compiler_params=pltpu.CompilerParams(
            collective_id=0, has_side_effects=True, vmem_limit_bytes=60 * 1024 * 1024
        ),
    )(
        gate_act, up_act, codes, scales,
        local_padded(HAD_LOCAL), walsh,
        swap_table(blocks, ranks), swap_table(rows, blocks), swap_table(chunks, rows),
    )
    return out.reshape(1, width)


def choose(gate_act, up_act, codes, scales):
    groups, ranks = lax.axis_size("groups"), lax.axis_size("tensor")
    fused = (
        gate_act.shape[0] // HAD_LOCAL % 8 == 0
        and gate_act.shape[1] == ranks
        and codes.shape[1] % (groups * CHUNK * 8) == 0
    )
    return (fused_body if fused else body)(gate_act, up_act, codes, scales)


def solution(mesh):
    placed = (P("tensor", "groups"), P("tensor", "groups"), P("tensor", None), P("tensor", None))
    return jax.shard_map(
        choose, mesh=mesh, in_specs=placed, out_specs=P(("groups", "tensor"), None), check_vma=False
    )
```

```python
import functools
import math

import jax
import jax.numpy as jnp
import numpy as np
from jax import lax
from jax.experimental import pallas as pl
from jax.experimental.pallas import tpu as pltpu
from jax.sharding import PartitionSpec as P

HAD_CROSS = 128
GROUP = 32
HAD_LOCAL = 416


def swapped(value, axis, distance):
    mask = 2**distance
    pairs = [(source, source ^ mask) for source in range(lax.axis_size(axis))]
    return lax.ppermute(value, axis, pairs)


def paley_table():
    squares = set()
    for real_part in range(5):
        for root_part in range(5):
            squares.add(
                (
                    (real_part * real_part + 2 * root_part * root_part) % 5,
                    2 * real_part * root_part % 5,
                )
            )
    jacobsthal = np.zeros((25, 25))
    for first in range(25):
        for second in range(25):
            differ = ((first // 5 - second // 5) % 5, (first % 5 - second % 5) % 5)
            if differ == (0, 0):
                jacobsthal[first, second] = 0.0
            elif differ in squares:
                jacobsthal[first, second] = 1.0
            else:
                jacobsthal[first, second] = -1.0
    conference = np.zeros((26, 26))
    conference[0, 1:] = 1.0
    conference[1:, 0] = 1.0
    conference[1:, 1:] = jacobsthal
    return np.kron(conference, np.array([[1.0, 1.0], [1.0, -1.0]])) + np.kron(
        np.eye(26), np.array([[1.0, -1.0], [-1.0, -1.0]])
    )


def walsh_table(order):
    matrix = np.ones((1, 1))
    while matrix.shape[0] < order:
        matrix = np.kron(np.array([[1.0, 1.0], [1.0, -1.0]]), matrix)
    return matrix


def hadamard_local(order):
    matrix = np.kron(walsh_table(order // 52), paley_table()) / math.sqrt(order)
    return jnp.asarray(matrix, dtype=jnp.float32).astype(jnp.bfloat16)


def sign_table(order):
    row_index = jnp.arange(order, dtype=jnp.int32)[:, None]
    col_index = jnp.arange(order, dtype=jnp.int32)[None, :]
    shared = jnp.zeros((order, order), jnp.int32)
    for bit_pos in range(order.bit_length() - 1):
        shared = shared + row_index // 2**bit_pos % 2 * (col_index // 2**bit_pos % 2)
    return (1 - 2 * (shared % 2)).astype(jnp.float32)


def dequantize(words, group_scales):
    low_codes = words % 16
    high_codes = words // 16
    unpacked = jnp.stack([low_codes, high_codes], axis=1).reshape(
        2 * words.shape[0], words.shape[1]
    )
    spread = jnp.repeat(group_scales.astype(jnp.float32), GROUP, axis=0)
    return ((unpacked - 8).astype(jnp.float32) * spread).astype(jnp.bfloat16)


def body(gate_act, up_act, codes, scales):
    units_here = gate_act.shape[0]
    total_rows = gate_act.shape[1]
    blocks_here = units_here // HAD_LOCAL
    factor = 1.0 / math.sqrt(HAD_CROSS)
    hidden = (jax.nn.silu(gate_act.astype(jnp.float32)) * up_act.astype(jnp.float32)).astype(
        jnp.bfloat16
    )
    hidden = hidden.reshape(blocks_here, HAD_LOCAL, total_rows)
    local_table = hadamard_local(HAD_LOCAL)
    local = jnp.einsum(
        "kn,anr->akr", local_table, hidden, preferred_element_type=jnp.float32
    ).astype(jnp.bfloat16)
    partial_sums = jnp.einsum(
        "abr,ae->ebr",
        local.astype(jnp.float32),
        sign_table(blocks_here),
        precision=lax.Precision.HIGHEST,
    )
    my_index = lax.axis_index("tensor")
    for bit_pos in range(lax.axis_size("tensor").bit_length() - 1):
        partner = swapped(partial_sums, "tensor", bit_pos)
        upper = my_index // 2**bit_pos % 2
        partial_sums = jnp.where(upper == 0, partial_sums + partner, partner - partial_sums)
    rotated = (partial_sums * factor).astype(jnp.bfloat16)
    rotated = rotated.reshape(units_here, total_rows)
    weight = dequantize(codes, scales)
    summed = lax.psum_scatter(
        lax.dot_general(
            rotated, weight, (((0,), (0,)), ((), ())), preferred_element_type=jnp.float32
        ),
        "tensor",
        scatter_dimension=0,
        tiled=True,
    )
    return summed.astype(jnp.bfloat16)


MESH = pl.DeviceIdType.MESH
CHUNK = 512
PAD = 512
PARTS = 2
SPLITS = (2, 5)


def local_padded(order):
    matrix = np.kron(walsh_table(order // 52), paley_table()) / math.sqrt(order)
    half = order // 2
    table = np.zeros((order, PAD), np.float32)
    table[:, :half] = matrix[0::2].T
    table[:, half : 2 * half] = matrix[1::2].T
    return jnp.asarray(table).astype(jnp.bfloat16)


def swap_table(outer, inner):
    table = np.zeros((outer * inner, outer * inner), np.float32)
    for i in range(outer):
        for j in range(inner):
            table[j * outer + i, i * inner + j] = 1.0
    return jnp.asarray(table).astype(jnp.bfloat16)


def f32_dot(left, right):
    return jnp.dot(left, right, preferred_element_type=jnp.float32)


def fused_kernel(
    sizes,
    gate_ref, up_ref, codes_ref, scales_ref, table_ref, walsh_ref, swap1_ref, swap2_ref, swap3_ref,
    out_ref,
    words, weights, scale16, scale32, snd1, rcv1, snd2, rcv2, rot, acc, snd3, rcv3,
    code_sem, scale_sem, send1, recv1, send2, recv2, send3, recv3,
):
    groups, ranks, blocks, chunks = sizes
    rows = groups * ranks
    half_words = HAD_LOCAL // 2
    bands = HAD_LOCAL // GROUP
    band = GROUP // 2
    my_group = lax.axis_index("groups")
    my_rank = lax.axis_index("tensor")
    me = my_group * ranks + my_rank
    base = my_group * (chunks * CHUNK)

    def code_copy(j):
        start = pl.multiple_of(base + j * CHUNK, CHUNK)
        return pltpu.make_async_copy(
            codes_ref.at[:, pl.ds(start, CHUNK)], words.at[j], code_sem.at[j]
        )

    scale_copy = pltpu.make_async_copy(
        scales_ref.at[:, pl.ds(pl.multiple_of(base, CHUNK), chunks * CHUNK)], scale16, scale_sem
    )
    scale_copy.start()

    @pl.loop(0, chunks)
    def _(j):
        code_copy(j).start()

    barrier = pltpu.get_barrier_semaphore()

    @pl.loop(1, rows)
    def _(k):
        peer = lax.rem(me + k, rows)
        pl.semaphore_signal(
            barrier, inc=1, device_id=(peer // ranks, lax.rem(peer, ranks)), device_id_type=MESH
        )

    def dequantize_chunk(j):
        code_copy(j).wait()
        columns = pl.ds(pl.multiple_of(j * CHUNK, CHUNK), CHUNK)
        for a in range(blocks):
            for n in range(bands):
                word = words[j, a * half_words + n * band : a * half_words + (n + 1) * band, :]
                row = a * bands + n
                scale = jnp.broadcast_to(scale32[row : row + 1, columns], (band, CHUNK)).astype(
                    jnp.bfloat16
                )
                low = ((word & 15).astype(jnp.float32).astype(jnp.bfloat16) - 8) * scale
                high = ((word >> 4).astype(jnp.float32).astype(jnp.bfloat16) - 8) * scale
                at = a * HAD_LOCAL + n * band
                weights[j, at : at + band, :] = low
                weights[j, at + half_words : at + half_words + band, :] = high

    def dequantize_chunks(first, last):
        @pl.loop(first, last)
        def _(j):
            dequantize_chunk(j)

    gate = gate_ref[...].astype(jnp.float32)
    hidden = (gate / (1.0 + jnp.exp(-gate)) * up_ref[...].astype(jnp.float32)).astype(jnp.bfloat16)
    stacked = jnp.concatenate(
        [hidden[:, a * HAD_LOCAL : (a + 1) * HAD_LOCAL] for a in range(blocks)], axis=0
    )
    parts = [f32_dot(stacked, table_ref[...]).astype(jnp.bfloat16)]
    local = f32_dot(swap1_ref[...], jnp.concatenate(parts, axis=0))
    snd1[...] = local.reshape(ranks, blocks, PAD).astype(jnp.bfloat16)
    rcv1[my_rank] = snd1[my_rank]
    scale_copy.wait()
    scale32[...] = scale16[...].astype(jnp.float32)
    dequantize_chunks(0, SPLITS[0])
    pl.semaphore_wait(barrier, rows - 1)

    def copy1(k):
        peer = lax.rem(my_rank + k, ranks)
        return pltpu.make_async_remote_copy(
            src_ref=snd1.at[peer], dst_ref=rcv1.at[my_rank],
            send_sem=send1.at[k], recv_sem=recv1.at[k],
            device_id=(my_group, peer), device_id_type=MESH,
        )

    @pl.loop(1, ranks)
    def _(k):
        copy1(k).start()

    dequantize_chunks(SPLITS[0], SPLITS[1])

    @pl.loop(1, ranks)
    def _(k):
        copy1(k).wait()

    gathered = rcv1[...].astype(jnp.float32).reshape(ranks * blocks, PAD).astype(jnp.bfloat16)
    rotated = f32_dot(walsh_ref[...], gathered) * (1.0 / math.sqrt(HAD_CROSS))
    snd2[...] = rotated.reshape(ranks, blocks, PAD).astype(jnp.bfloat16)
    rcv2[me] = snd2[my_rank]

    def copy2(k):
        peer = lax.rem(me + k, rows)
        return pltpu.make_async_remote_copy(
            src_ref=snd2.at[lax.rem(peer, ranks)], dst_ref=rcv2.at[me],
            send_sem=send2.at[k], recv_sem=recv2.at[k],
            device_id=(peer // ranks, lax.rem(peer, ranks)), device_id_type=MESH,
        )

    @pl.loop(1, rows)
    def _(k):
        copy2(k).start()

    dequantize_chunks(SPLITS[1], chunks)

    @pl.loop(1, rows)
    def _(k):
        copy2(k).wait()

    gathered = rcv2[...].astype(jnp.float32).reshape(rows * blocks, PAD).astype(jnp.bfloat16)
    ordered = f32_dot(swap2_ref[...], gathered).astype(jnp.bfloat16)
    rot[...] = jnp.concatenate(
        [ordered[a * rows : (a + 1) * rows, :HAD_LOCAL] for a in range(blocks)], axis=1
    )

    def copy3(part, k):
        peer = lax.rem(me + k, rows)
        return pltpu.make_async_remote_copy(
            src_ref=snd3.at[part, peer], dst_ref=rcv3.at[part, me],
            send_sem=send3.at[part, k], recv_sem=recv3.at[part, k],
            device_id=(peer // ranks, lax.rem(peer, ranks)), device_id_type=MESH,
        )

    fold = chunks // PARTS
    width = fold * CHUNK // 8
    for part in range(PARTS):
        @pl.loop(0, fold)
        def _(j):
            total = f32_dot(rot[...], weights[part * fold + j]).astype(jnp.bfloat16)
            for n in range(CHUNK // width):
                at = pl.multiple_of((j * (CHUNK // width) + n) * rows, rows)
                acc[pl.ds(at, rows), :] = total[:, n * width : (n + 1) * width]

        sums = f32_dot(swap3_ref[...], acc[...])
        snd3[part] = sums.reshape(rows, 8, width).astype(jnp.bfloat16)
        rcv3[part, me] = snd3[part, me]

        @pl.loop(1, rows)
        def _(k):
            copy3(part, k).start()

    for part in range(PARTS):
        @pl.loop(1, rows)
        def _(k):
            copy3(part, k).wait()

        for g in range(groups):
            out_ref[g, part] = jnp.sum(
                rcv3[part, g * ranks : (g + 1) * ranks].astype(jnp.float32), axis=0
            ).astype(jnp.bfloat16)


def fused_body(gate_act, up_act, codes, scales):
    groups, ranks = lax.axis_size("groups"), lax.axis_size("tensor")
    rows = groups * ranks
    blocks = gate_act.shape[0] // HAD_LOCAL
    width = codes.shape[1]
    chunks = width // groups // CHUNK
    part_width = width // groups // PARTS // 8
    vmem = pl.BlockSpec(memory_space=pltpu.VMEM)
    hbm = pl.BlockSpec(memory_space=pl.ANY)
    bf16 = jnp.bfloat16
    walsh = jnp.asarray(walsh_table(HAD_CROSS), jnp.float32).astype(bf16)
    out = pl.pallas_call(
        functools.partial(fused_kernel, (groups, ranks, blocks, chunks)),
        out_shape=jax.ShapeDtypeStruct((groups, PARTS, 8, part_width), bf16),
        in_specs=[vmem, vmem, hbm, hbm] + [vmem] * 5,
        out_specs=vmem,
        scratch_shapes=[
            pltpu.VMEM((chunks, codes.shape[0], CHUNK), jnp.int32),
            pltpu.VMEM((chunks, 2 * codes.shape[0], CHUNK), bf16),
            pltpu.VMEM((scales.shape[0], chunks * CHUNK), bf16),
            pltpu.VMEM((scales.shape[0], chunks * CHUNK), jnp.float32),
            pltpu.VMEM((ranks, blocks, PAD), bf16),
            pltpu.VMEM((ranks, blocks, PAD), bf16),
            pltpu.VMEM((ranks, blocks, PAD), bf16),
            pltpu.VMEM((rows, blocks, PAD), bf16),
            pltpu.VMEM((rows, 2 * codes.shape[0]), bf16),
            pltpu.VMEM((8 * rows, part_width), bf16),
            pltpu.VMEM((PARTS, rows, 8, part_width), bf16),
            pltpu.VMEM((PARTS, rows, 8, part_width), bf16),
            pltpu.SemaphoreType.DMA((chunks,)),
            pltpu.SemaphoreType.DMA,
            pltpu.SemaphoreType.DMA((ranks,)),
            pltpu.SemaphoreType.DMA((ranks,)),
            pltpu.SemaphoreType.DMA((rows,)),
            pltpu.SemaphoreType.DMA((rows,)),
            pltpu.SemaphoreType.DMA((PARTS, rows)),
            pltpu.SemaphoreType.DMA((PARTS, rows)),
        ],
        compiler_params=pltpu.CompilerParams(
            collective_id=0, has_side_effects=True, vmem_limit_bytes=67043328
        ),
    )(
        gate_act.T, up_act.T, codes, scales,
        local_padded(HAD_LOCAL), walsh,
        swap_table(blocks, ranks), swap_table(rows, blocks), swap_table(8, rows),
    )
    return out.reshape(1, width)


def choose(gate_act, up_act, codes, scales):
    groups, ranks = lax.axis_size("groups"), lax.axis_size("tensor")
    fused = (
        gate_act.shape[0] // HAD_LOCAL % 8 == 0
        and gate_act.shape[1] == ranks
        and codes.shape[1] % (groups * CHUNK * 8) == 0
    )
    return (fused_body if fused else body)(gate_act, up_act, codes, scales)


def solution(mesh):
    placed = (P("tensor", "groups"), P("tensor", "groups"), P("tensor", None), P("tensor", None))
    return jax.shard_map(
        choose, mesh=mesh, in_specs=placed, out_specs=P(("groups", "tensor"), None), check_vma=False
    )
```

```python
import functools
import math

import jax
import jax.numpy as jnp
import numpy as np
from jax import lax
from jax.experimental import pallas as pl
from jax.experimental.pallas import tpu as pltpu
from jax.sharding import PartitionSpec as P

HAD_CROSS = 128
GROUP = 32
HAD_LOCAL = 416


def swapped(value, axis, distance):
    mask = 2**distance
    pairs = [(source, source ^ mask) for source in range(lax.axis_size(axis))]
    return lax.ppermute(value, axis, pairs)


def paley_table():
    squares = set()
    for real_part in range(5):
        for root_part in range(5):
            squares.add(
                (
                    (real_part * real_part + 2 * root_part * root_part) % 5,
                    2 * real_part * root_part % 5,
                )
            )
    jacobsthal = np.zeros((25, 25))
    for first in range(25):
        for second in range(25):
            differ = ((first // 5 - second // 5) % 5, (first % 5 - second % 5) % 5)
            if differ == (0, 0):
                jacobsthal[first, second] = 0.0
            elif differ in squares:
                jacobsthal[first, second] = 1.0
            else:
                jacobsthal[first, second] = -1.0
    conference = np.zeros((26, 26))
    conference[0, 1:] = 1.0
    conference[1:, 0] = 1.0
    conference[1:, 1:] = jacobsthal
    return np.kron(conference, np.array([[1.0, 1.0], [1.0, -1.0]])) + np.kron(
        np.eye(26), np.array([[1.0, -1.0], [-1.0, -1.0]])
    )


def walsh_table(order):
    matrix = np.ones((1, 1))
    while matrix.shape[0] < order:
        matrix = np.kron(np.array([[1.0, 1.0], [1.0, -1.0]]), matrix)
    return matrix


def hadamard_local(order):
    matrix = np.kron(walsh_table(order // 52), paley_table()) / math.sqrt(order)
    return jnp.asarray(matrix, dtype=jnp.float32).astype(jnp.bfloat16)


def sign_table(order):
    row_index = jnp.arange(order, dtype=jnp.int32)[:, None]
    col_index = jnp.arange(order, dtype=jnp.int32)[None, :]
    shared = jnp.zeros((order, order), jnp.int32)
    for bit_pos in range(order.bit_length() - 1):
        shared = shared + row_index // 2**bit_pos % 2 * (col_index // 2**bit_pos % 2)
    return (1 - 2 * (shared % 2)).astype(jnp.float32)


def dequantize(words, group_scales):
    low_codes = words % 16
    high_codes = words // 16
    unpacked = jnp.stack([low_codes, high_codes], axis=1).reshape(
        2 * words.shape[0], words.shape[1]
    )
    spread = jnp.repeat(group_scales.astype(jnp.float32), GROUP, axis=0)
    return ((unpacked - 8).astype(jnp.float32) * spread).astype(jnp.bfloat16)


def body(gate_act, up_act, codes, scales):
    units_here = gate_act.shape[0]
    total_rows = gate_act.shape[1]
    blocks_here = units_here // HAD_LOCAL
    factor = 1.0 / math.sqrt(HAD_CROSS)
    hidden = (jax.nn.silu(gate_act.astype(jnp.float32)) * up_act.astype(jnp.float32)).astype(
        jnp.bfloat16
    )
    hidden = hidden.reshape(blocks_here, HAD_LOCAL, total_rows)
    local_table = hadamard_local(HAD_LOCAL)
    local = jnp.einsum(
        "kn,anr->akr", local_table, hidden, preferred_element_type=jnp.float32
    ).astype(jnp.bfloat16)
    partial_sums = jnp.einsum(
        "abr,ae->ebr",
        local.astype(jnp.float32),
        sign_table(blocks_here),
        precision=lax.Precision.HIGHEST,
    )
    my_index = lax.axis_index("tensor")
    for bit_pos in range(lax.axis_size("tensor").bit_length() - 1):
        partner = swapped(partial_sums, "tensor", bit_pos)
        upper = my_index // 2**bit_pos % 2
        partial_sums = jnp.where(upper == 0, partial_sums + partner, partner - partial_sums)
    rotated = (partial_sums * factor).astype(jnp.bfloat16)
    rotated = rotated.reshape(units_here, total_rows)
    weight = dequantize(codes, scales)
    summed = lax.psum_scatter(
        lax.dot_general(
            rotated, weight, (((0,), (0,)), ((), ())), preferred_element_type=jnp.float32
        ),
        "tensor",
        scatter_dimension=0,
        tiled=True,
    )
    return summed.astype(jnp.bfloat16)


MESH = pl.DeviceIdType.MESH
CHUNK = 512
PAD = 512
PARTS = 2
SPLITS = (2, 4, 6)


def local_padded(order):
    matrix = np.kron(walsh_table(order // 52), paley_table()) / math.sqrt(order)
    half = order // 2
    table = np.zeros((order, PAD), np.float32)
    table[:, :half] = matrix[0::2].T
    table[:, half : 2 * half] = matrix[1::2].T
    return jnp.asarray(table).astype(jnp.bfloat16)


def swap_table(outer, inner):
    table = np.zeros((outer * inner, outer * inner), np.float32)
    for i in range(outer):
        for j in range(inner):
            table[j * outer + i, i * inner + j] = 1.0
    return jnp.asarray(table).astype(jnp.bfloat16)


def owner_table(pieces, rows):
    table = np.zeros((pieces * rows, pieces * rows), np.float32)
    for piece in range(pieces):
        for row in range(rows):
            place = row % 2 * (rows // 2) + row // 2
            table[place * pieces + piece, piece * rows + row] = 1.0
    return jnp.asarray(table).astype(jnp.bfloat16)


def f32_dot(left, right):
    return jnp.dot(left, right, preferred_element_type=jnp.float32)


def fused_kernel(
    sizes,
    gate_ref, up_ref, codes_ref, scales_ref, table_ref, walsh_ref, swap1_ref, swap2_ref, swap3_ref,
    out_ref,
    words, weights, scale16, scale32, snd1, rcv1, snd2, rcv2, rot, acc, snd3, half3, sum3, rcv3,
    code_sem, scale_sem, send1, recv1, send2, recv2, send3, recv3, send4, recv4, send5, recv5,
):
    groups, ranks, blocks, chunks = sizes
    rows = groups * ranks
    half_words = HAD_LOCAL // 2
    bands = HAD_LOCAL // GROUP
    band = GROUP // 2
    my_group = lax.axis_index("groups")
    my_rank = lax.axis_index("tensor")
    me = my_group * ranks + my_rank
    base = my_group * (chunks * CHUNK)

    def code_copy(j):
        start = pl.multiple_of(base + j * CHUNK, CHUNK)
        return pltpu.make_async_copy(
            codes_ref.at[:, pl.ds(start, CHUNK)], words.at[j], code_sem.at[j]
        )

    scale_copy = pltpu.make_async_copy(
        scales_ref.at[:, pl.ds(pl.multiple_of(base, CHUNK), chunks * CHUNK)], scale16, scale_sem
    )
    scale_copy.start()

    @pl.loop(0, chunks)
    def _(j):
        code_copy(j).start()

    barrier = pltpu.get_barrier_semaphore()

    @pl.loop(1, rows)
    def _(k):
        peer = lax.rem(me + k, rows)
        pl.semaphore_signal(
            barrier, inc=1, device_id=(peer // ranks, lax.rem(peer, ranks)), device_id_type=MESH
        )

    def dequantize_chunk(j):
        code_copy(j).wait()
        columns = pl.ds(pl.multiple_of(j * CHUNK, CHUNK), CHUNK)
        for a in range(blocks):
            for n in range(bands):
                word = words[j, a * half_words + n * band : a * half_words + (n + 1) * band, :]
                row = a * bands + n
                scale = jnp.broadcast_to(scale32[row : row + 1, columns], (band, CHUNK)).astype(
                    jnp.bfloat16
                )
                low = ((word & 15).astype(jnp.float32).astype(jnp.bfloat16) - 8) * scale
                high = ((word >> 4).astype(jnp.float32).astype(jnp.bfloat16) - 8) * scale
                at = a * HAD_LOCAL + n * band
                weights[j, at : at + band, :] = low
                weights[j, at + half_words : at + half_words + band, :] = high

    def dequantize_chunks(first, last):
        @pl.loop(first, last)
        def _(j):
            dequantize_chunk(j)

    gate = gate_ref[...].astype(jnp.float32)
    hidden = (gate / (1.0 + jnp.exp(-gate)) * up_ref[...].astype(jnp.float32)).astype(jnp.bfloat16)
    stacked = jnp.concatenate(
        [hidden[:, a * HAD_LOCAL : (a + 1) * HAD_LOCAL] for a in range(blocks)], axis=0
    )
    parts = [f32_dot(stacked, table_ref[...]).astype(jnp.bfloat16)]
    local = f32_dot(swap1_ref[...], jnp.concatenate(parts, axis=0))
    snd1[...] = local.reshape(ranks, blocks, PAD).astype(jnp.bfloat16)
    rcv1[my_rank] = snd1[my_rank]
    scale_copy.wait()
    scale32[...] = scale16[...].astype(jnp.float32)
    dequantize_chunks(0, SPLITS[0])
    pl.semaphore_wait(barrier, rows - 1)

    def copy1(k):
        peer = lax.rem(my_rank + k, ranks)
        return pltpu.make_async_remote_copy(
            src_ref=snd1.at[peer], dst_ref=rcv1.at[my_rank],
            send_sem=send1.at[k], recv_sem=recv1.at[k],
            device_id=(my_group, peer), device_id_type=MESH,
        )

    @pl.loop(1, ranks)
    def _(k):
        copy1(k).start()

    dequantize_chunks(SPLITS[0], SPLITS[1])

    @pl.loop(1, ranks)
    def _(k):
        copy1(k).wait()

    gathered = rcv1[...].astype(jnp.float32).reshape(ranks * blocks, PAD).astype(jnp.bfloat16)
    rotated = f32_dot(walsh_ref[...], gathered) * (1.0 / math.sqrt(HAD_CROSS))
    snd2[...] = rotated.reshape(ranks, blocks, PAD).astype(jnp.bfloat16)
    rcv2[me] = snd2[my_rank]

    def copy2(k):
        peer = lax.rem(my_rank + k, ranks)
        return pltpu.make_async_remote_copy(
            src_ref=snd2.at[peer], dst_ref=rcv2.at[me],
            send_sem=send2.at[k], recv_sem=recv2.at[k],
            device_id=(my_group, peer), device_id_type=MESH,
        )

    def forward(k):
        slot = my_group * ranks + lax.rem(my_rank + ranks - k, ranks)
        return pltpu.make_async_remote_copy(
            src_ref=rcv2.at[slot], dst_ref=rcv2.at[slot],
            send_sem=send4.at[k], recv_sem=recv4.at[k],
            device_id=(1 - my_group, my_rank), device_id_type=MESH,
        )

    @pl.loop(1, ranks)
    def _(k):
        copy2(k).start()

    forward(0).start()
    dequantize_chunks(SPLITS[1], SPLITS[2])

    @pl.loop(1, ranks)
    def _(k):
        copy2(k).wait_recv()
        forward(k).start()

    dequantize_chunks(SPLITS[2], chunks)

    @pl.loop(1, ranks)
    def _(k):
        copy2(k).wait_send()

    @pl.loop(0, ranks)
    def _(k):
        forward(k).wait()

    gathered = rcv2[...].astype(jnp.float32).reshape(rows * blocks, PAD).astype(jnp.bfloat16)
    ordered = f32_dot(swap2_ref[...], gathered).astype(jnp.bfloat16)
    rot[...] = jnp.concatenate(
        [ordered[a * rows : (a + 1) * rows, :HAD_LOCAL] for a in range(blocks)], axis=1
    )

    cores = 2
    my_core = lax.rem(my_rank, cores)
    kin = rows // cores
    spots = ranks // cores
    my_spot = my_group * spots + my_rank // cores

    def pair(part):
        return pltpu.make_async_remote_copy(
            src_ref=snd3.at[part, 1 - my_core], dst_ref=half3.at[part],
            send_sem=send5.at[part], recv_sem=recv5.at[part],
            device_id=(my_group, my_rank + 1 - 2 * my_core), device_id_type=MESH,
        )

    def copy3(part, k):
        peer = lax.rem(my_spot + k, kin)
        return pltpu.make_async_remote_copy(
            src_ref=sum3.at[part, peer], dst_ref=rcv3.at[part, my_spot],
            send_sem=send3.at[part, k], recv_sem=recv3.at[part, k],
            device_id=(peer // spots, lax.rem(peer, spots) * cores + my_core),
            device_id_type=MESH,
        )

    fold = chunks // PARTS
    width = fold * CHUNK // 8
    for part in range(PARTS + 1):
        if part < PARTS:
            @pl.loop(0, fold)
            def _(j):
                total = f32_dot(rot[...], weights[part * fold + j]).astype(jnp.bfloat16)
                for n in range(CHUNK // width):
                    at = pl.multiple_of((j * (CHUNK // width) + n) * rows, rows)
                    acc[pl.ds(at, rows), :] = total[:, n * width : (n + 1) * width]

            sums = f32_dot(swap3_ref[...], acc[...])
            snd3[part] = sums.reshape(cores, kin, 8, width).astype(jnp.bfloat16)
            pair(part).start()
        if part > 0:
            pair(part - 1).wait()
            sum3[part - 1] = (
                snd3[part - 1, my_core].astype(jnp.float32) + half3[part - 1].astype(jnp.float32)
            ).astype(jnp.bfloat16)
            rcv3[part - 1, my_spot] = sum3[part - 1, my_spot]

            @pl.loop(1, kin)
            def _(k):
                copy3(part - 1, k).start()

    for part in range(PARTS):
        @pl.loop(1, kin)
        def _(k):
            copy3(part, k).wait()

        for g in range(groups):
            total = jnp.sum(
                rcv3[part, g * spots : (g + 1) * spots].astype(jnp.float32), axis=0
            ).astype(jnp.bfloat16)
            for n in range(8):
                at = ((g * PARTS + part) * 8 + n) * width
                out_ref[:, at : at + width] = total[n : n + 1]


def fused_body(gate_act, up_act, codes, scales):
    groups, ranks = lax.axis_size("groups"), lax.axis_size("tensor")
    rows = groups * ranks
    blocks = gate_act.shape[0] // HAD_LOCAL
    width = codes.shape[1]
    chunks = width // groups // CHUNK
    part_width = width // groups // PARTS // 8
    vmem = pl.BlockSpec(memory_space=pltpu.VMEM)
    hbm = pl.BlockSpec(memory_space=pl.ANY)
    bf16 = jnp.bfloat16
    walsh = jnp.asarray(walsh_table(HAD_CROSS), jnp.float32).astype(bf16)
    out = pl.pallas_call(
        functools.partial(fused_kernel, (groups, ranks, blocks, chunks)),
        out_shape=jax.ShapeDtypeStruct((1, width), bf16),
        in_specs=[vmem, vmem, hbm, hbm] + [vmem] * 5,
        out_specs=vmem,
        scratch_shapes=[
            pltpu.VMEM((chunks, codes.shape[0], CHUNK), jnp.int32),
            pltpu.VMEM((chunks, 2 * codes.shape[0], CHUNK), bf16),
            pltpu.VMEM((scales.shape[0], chunks * CHUNK), bf16),
            pltpu.VMEM((scales.shape[0], chunks * CHUNK), jnp.float32),
            pltpu.VMEM((ranks, blocks, PAD), bf16),
            pltpu.VMEM((ranks, blocks, PAD), bf16),
            pltpu.VMEM((ranks, blocks, PAD), bf16),
            pltpu.VMEM((rows, blocks, PAD), bf16),
            pltpu.VMEM((rows, 2 * codes.shape[0]), bf16),
            pltpu.VMEM((8 * rows, part_width), bf16),
            pltpu.VMEM((PARTS, 2, rows // 2, 8, part_width), bf16),
            pltpu.VMEM((PARTS, rows // 2, 8, part_width), bf16),
            pltpu.VMEM((PARTS, rows // 2, 8, part_width), bf16),
            pltpu.VMEM((PARTS, rows // 2, 8, part_width), bf16),
            pltpu.SemaphoreType.DMA((chunks,)),
            pltpu.SemaphoreType.DMA,
            pltpu.SemaphoreType.DMA((ranks,)),
            pltpu.SemaphoreType.DMA((ranks,)),
            pltpu.SemaphoreType.DMA((ranks,)),
            pltpu.SemaphoreType.DMA((ranks,)),
            pltpu.SemaphoreType.DMA((PARTS, rows // 2)),
            pltpu.SemaphoreType.DMA((PARTS, rows // 2)),
            pltpu.SemaphoreType.DMA((ranks,)),
            pltpu.SemaphoreType.DMA((ranks,)),
            pltpu.SemaphoreType.DMA((PARTS,)),
            pltpu.SemaphoreType.DMA((PARTS,)),
        ],
        compiler_params=pltpu.CompilerParams(
            collective_id=0, has_side_effects=True, vmem_limit_bytes=67043328
        ),
    )(
        gate_act.T, up_act.T, codes, scales,
        local_padded(HAD_LOCAL), walsh,
        swap_table(blocks, ranks), swap_table(rows, blocks), owner_table(8, rows),
    )
    return out


def choose(gate_act, up_act, codes, scales):
    groups, ranks = lax.axis_size("groups"), lax.axis_size("tensor")
    fused = (
        gate_act.shape[0] // HAD_LOCAL % 8 == 0
        and gate_act.shape[1] == ranks
        and groups == 2
        and ranks % 2 == 0
        and codes.shape[1] % (groups * CHUNK * 8) == 0
    )
    return (fused_body if fused else body)(gate_act, up_act, codes, scales)


def solution(mesh):
    placed = (P("tensor", "groups"), P("tensor", "groups"), P("tensor", None), P("tensor", None))
    return jax.shard_map(
        choose, mesh=mesh, in_specs=placed, out_specs=P(("groups", "tensor"), None), check_vma=False
    )
```
